32 devices in a mesh: seq: 4 (over x, core), fsdp: 8 (over z, y).
Axes of the slice: x: 2, y: 2, z: 4, core: 2. Of those that a mesh axis runs over, the one named last changes fastest.
Arguments:
- hidden_in: bfloat16 [8, 512, 1024], P('fsdp', 'seq'), may hold values from -6 to 6
- grad_out: bfloat16 [8, 512, 1024], P('fsdp', 'seq'), may hold values from -6 to 6
- segments: int32 [8, 512], P('fsdp'), may hold values from 0 to 1, as said below
- norm_gain: bfloat16 [1024], P('fsdp'), may hold values from 0.5 to 1.5
- mamba_in: bfloat16 [1024, 3328], P('fsdp'), may hold values from -0.1875 to 0.1875
- step_in: bfloat16 [1024, 24], P('fsdp'), may hold values from -0.1875 to 0.1875
- attn_in: bfloat16 [1024, 768], P('fsdp'), may hold values from -0.1875 to 0.1875
- conv_taps: float32 [4, 1792], replicated, may hold values from -3 to 3
- conv_bias: float32 [1792], replicated, may hold values from -1.75 to 1.75
- step_bias: float32 [24], replicated, may hold values from -2 to 0.5
- log_decay: float32 [24], replicated, may hold values from -7 to -2.5
- skip_gain: float32 [24], replicated, may hold values from 0.5 to 1.5
- gated_gain: bfloat16 [1536], P('fsdp'), may hold values from 0.5 to 1.5
- mamba_out: bfloat16 [1536, 1024], P('fsdp'), may hold values from -0.15625 to 0.15625
- attn_out: bfloat16 [512, 1024], P('fsdp'), may hold values from -0.75 to 0.75
- ffn_gain: bfloat16 [1024], P('fsdp'), may hold values from 0.5 to 1.5
- gate_up: bfloat16 [1024, 4096], P('fsdp'), may hold values from -0.1875 to 0.1875
- down_proj: bfloat16 [2048, 1024], P('fsdp'), may hold values from -0.125 to 0.125
Outputs:
- hidden_out: bfloat16 [8, 512, 1024], P('fsdp', 'seq')
- grad_in: float32 [8, 512, 1024], P('fsdp', 'seq')
- grad_norm_gain: float32 [1024], P('fsdp')
- grad_mamba_in: float32 [1024, 3328], P('fsdp')
- grad_step_in: float32 [1024, 24], P('fsdp')
- grad_attn_in: float32 [1024, 768], P('fsdp')
- grad_conv_taps: float32 [4, 1792], replicated
- grad_conv_bias: float32 [1792], replicated
- grad_step_bias: float32 [24], replicated
- grad_log_decay: float32 [24], replicated
- grad_skip_gain: float32 [24], replicated
- grad_gated_gain: float32 [1536], P('fsdp')
- grad_mamba_out: float32 [1536, 1024], P('fsdp')
- grad_attn_out: float32 [512, 1024], P('fsdp')
- grad_ffn_gain: float32 [1024], P('fsdp')
- grad_gate_up: float32 [1024, 4096], P('fsdp')
- grad_down_proj: float32 [2048, 1024], P('fsdp')
The draws below stay inside these ranges and needn't reach their ends.
Inputs may be any that keep to these rules, and one draw needn't show every extreme that they name: `segments`: in each pack the ids are 0 up to some position and 1 from there on: a pack holds one sequence or two, the first at least 128 tokens long.
All inputs are finite; a program needn't handle non-finite values.
Results may differ from the reference program's by a relative error of at most 0.015.
Values may be sent and summed in bfloat16 or wider, within the bound.
A program may use at most 192 MiB of HBM per device.

```python
import math
from functools import partial
import jax
import jax.numpy as jnp
from jax import lax

D = 1024
MH = 24
HD = 64
NST = 128
KC = 4
QH = 8
KVH = 2
FF = 2048
SPAN = 128
DI = 1536
LEN = 512
NPACK = 8
CONV_CH = 1792
N_SEQ = 4


def draw_segments(key, part):
    cut_at = jax.random.randint(key, (NPACK, 1), LEN // 4, LEN + LEN // 4)
    places = jnp.arange(LEN, dtype=jnp.int32)[None, :]
    return (places >= cut_at).astype(jnp.int32)


def steps_of(stream_key, shape, cuts, low, largest):
    factor_of = 1.0
    for axis_at, blocks in cuts:
        steps = jax.random.uniform(jax.random.fold_in(jax.random.fold_in(stream_key, 6), axis_at), (blocks,), jnp.float32, low / len(cuts), largest / len(cuts))
        factor_of = factor_of * jnp.repeat(jnp.exp(steps), shape[axis_at] // blocks).reshape((-1,) + (1,) * (len(shape) - 1 - axis_at))
    return factor_of


def scatter_about(rng, extent, deviation, reach, pieces=(), held_as=jnp.bfloat16):
    factor_of = steps_of(rng, extent, pieces, -0.22, 0.18) if pieces else 1.0
    result = jax.random.normal(rng, extent, jnp.float32) * deviation * factor_of
    return jnp.minimum(jnp.maximum(result, -reach), reach).astype(held_as)


def setup_inputs(seed: int = 0) -> dict:
    key_of = jax.random.split(jax.random.key(seed), 19)
    return {
        "hidden_in": scatter_about(key_of[0], (NPACK, LEN, D), 1.0, 6.0, ((0, 8), (1, 4))),
        "grad_out": scatter_about(key_of[1], (NPACK, LEN, D), 1.0, 6.0, ((0, 8), (1, 4))),
        "segments": draw_segments(jax.random.fold_in(key_of[18], 71), 0),
        "norm_gain": jnp.clip(1.0 + 0.1 * jax.random.normal(key_of[3], (D,), jnp.float32), 0.5, 1.5).astype(jnp.bfloat16),
        "mamba_in": scatter_about(key_of[4], (D, 2 * DI + 2 * NST), D ** -0.5, 0.1875, ((0, 8),)),
        "step_in": scatter_about(key_of[5], (D, MH), D ** -0.5, 0.1875, ((0, 8),)),
        "attn_in": scatter_about(key_of[6], (D, (QH + 2 * KVH) * HD), D ** -0.5, 0.1875, ((0, 8),)),
        "conv_taps": scatter_about(key_of[7], (KC, CONV_CH), 0.5, 3.0, (), jnp.float32),
        "conv_bias": scatter_about(key_of[8], (CONV_CH,), 0.3, 1.75, (), jnp.float32),
        "step_bias": jnp.clip(jax.random.uniform(key_of[9], (MH,), jnp.float32, -2.0, 0.5), -2.0, 0.5),
        "log_decay": jnp.clip(jax.random.uniform(key_of[10], (MH,), jnp.float32, -7.0, -2.5), -7.0, -2.5),
        "skip_gain": jnp.clip(jax.random.uniform(key_of[11], (MH,), jnp.float32, 0.5, 1.5), 0.5, 1.5),
        "gated_gain": jnp.clip(1.0 + 0.1 * jax.random.normal(key_of[12], (DI,), jnp.float32), 0.5, 1.5).astype(jnp.bfloat16),
        "mamba_out": scatter_about(key_of[13], (DI, D), DI ** -0.5, 0.15625, ((0, 8),)),
        "attn_out": scatter_about(key_of[14], (QH * HD, D), HD ** -0.5, 0.75, ((0, 8),)),
        "ffn_gain": jnp.clip(1.0 + 0.1 * jax.random.normal(key_of[15], (D,), jnp.float32), 0.5, 1.5).astype(jnp.bfloat16),
        "gate_up": scatter_about(key_of[16], (D, 2 * FF), D ** -0.5, 0.1875, ((0, 8),)),
        "down_proj": scatter_about(key_of[17], (FF, D), FF ** -0.5, 0.125, ((0, 8),)),
    }


EPS = 1e-05
ROPE_THETA = 10000.0

def rms_scale(values):
    return lax.rsqrt(lax.optimization_barrier(jnp.mean(values * values, axis=-1, keepdims=True)) + EPS)

def swish_slope(values):
    sigma = jax.nn.sigmoid(values)
    return sigma * (1.0 + values * (1.0 - sigma))

def scan_blocks(x_heads, b_mat, c_mat, step, log_step, seg_ids):
    row_count, head_count, width = x_heads.shape
    state = b_mat.shape[1]
    block_count = row_count // SPAN
    highest = lax.Precision.HIGHEST
    spots = jnp.arange(SPAN, dtype=jnp.int32)
    causal = spots[:, None] >= spots[None, :]

    def one_block(carry, items):
        state_in, prev_seg = carry
        x_blk, b_blk, c_blk, step_blk, log_blk, seg_blk = items
        local = jnp.cumsum(log_blk, axis=0)
        inside = causal & (seg_blk[:, None] == seg_blk[None, :])
        inner = jnp.dot(c_blk, b_blk.T, precision=highest)
        local_t = local.T
        expo = jnp.where(inside[None], local_t[:, :, None] - local_t[:, None, :], -1e+30)
        mixing = inner[None] * jnp.exp(expo) * step_blk.T[:, None, :]
        intra = jnp.einsum('htp,phd->thd', mixing, x_blk, precision=highest)
        carried = jnp.einsum('tn,hnd->thd', c_blk, state_in, precision=highest)
        lead = jnp.where((seg_blk == prev_seg)[:, None], jnp.exp(local), 0.0)
        out_blk = intra + lead[:, :, None] * carried
        last_seg = seg_blk[SPAN - 1]
        tail = jnp.where((seg_blk == last_seg)[:, None], jnp.exp(local[SPAN - 1][None, :] - local) * step_blk, 0.0)
        fresh = jnp.einsum('ph,pn,phd->hnd', tail, b_blk, x_blk, precision=highest)
        keep = jnp.where(prev_seg == last_seg, jnp.exp(local[SPAN - 1]), 0.0)
        state_out = keep[:, None, None] * state_in + fresh
        return ((state_out, last_seg), out_blk)
    start = (jnp.zeros((head_count, state, width), x_heads.dtype), jnp.int32(-1))
    items = (x_heads.reshape(block_count, SPAN, head_count, width), b_mat.reshape(block_count, SPAN, state), c_mat.reshape(block_count, SPAN, state), step.reshape(block_count, SPAN, head_count), log_step.reshape(block_count, SPAN, head_count), seg_ids.reshape(block_count, SPAN))
    final, outputs = lax.scan(one_block, start, items)
    return outputs.reshape(row_count, head_count, width)

def mixer_core(xs_in, bc_in, step_raw, query_in, kv_in, seg_ids, taps, tap_bias, step_bias, log_decay, skip_gain):
    row_count = xs_in.shape[0]
    head_count = step_raw.shape[1]
    width = xs_in.shape[1] // head_count
    state = bc_in.shape[1] // 2
    highest = lax.Precision.HIGHEST
    pre_conv = jnp.concatenate([xs_in, bc_in], axis=1)
    tap_count = taps.shape[0]
    accum = tap_bias[None, :] + taps[tap_count - 1][None, :] * pre_conv
    for lag_step in range(1, tap_count):
        moved = jnp.concatenate([jnp.zeros((lag_step, pre_conv.shape[1]), pre_conv.dtype), pre_conv[:row_count - lag_step]], axis=0)
        prior = jnp.concatenate([jnp.full((lag_step,), -1, jnp.int32), seg_ids[:row_count - lag_step]])
        same_seq = (prior == seg_ids)[:, None]
        accum = accum + taps[tap_count - 1 - lag_step][None, :] * jnp.where(same_seq, moved, 0.0)
    activated = jax.nn.silu(accum)
    x_heads = activated[:, :head_count * width].reshape(row_count, head_count, width)
    b_mat = activated[:, head_count * width:head_count * width + state]
    c_mat = activated[:, head_count * width + state:]
    step = jax.nn.softplus(step_raw + step_bias[None, :])
    log_step = -jnp.exp(log_decay)[None, :] * step
    ssm_out = scan_blocks(x_heads, b_mat, c_mat, step, log_step, seg_ids) + skip_gain[None, :, None] * x_heads
    positions = jnp.arange(row_count, dtype=jnp.int32)
    mask = (positions[:, None] >= positions[None, :]) & (seg_ids[:, None] == seg_ids[None, :])
    query_count = query_in.shape[1] // width
    kv_count = kv_in.shape[1] // (2 * width)
    group_size = query_count // kv_count
    place = (lax.optimization_barrier(jnp.sum(mask.astype(jnp.int32), axis=1)) - 1).astype(xs_in.dtype)
    half = width // 2
    freqs = jnp.exp(-math.log(ROPE_THETA) * 2.0 * jnp.arange(half, dtype=xs_in.dtype) / width)
    angles = place[:, None] * freqs[None, :]
    cosine = jnp.cos(angles)[:, None, :]
    sine = jnp.sin(angles)[:, None, :]

    def rotate(tensor):
        first_half = tensor[..., :half]
        second_half = tensor[..., half:]
        return jnp.concatenate([first_half * cosine - second_half * sine, second_half * cosine + first_half * sine], axis=-1)
    queries = rotate(query_in.reshape(row_count, query_count, width)).reshape(row_count, kv_count, group_size, width)
    kv_pair = kv_in.reshape(row_count, kv_count, 2, width)
    keys = rotate(kv_pair[:, :, 0])
    values = kv_pair[:, :, 1]
    scores = jnp.einsum('ikgp,jkp->kgij', queries, keys, precision=highest) * (1.0 / math.sqrt(width))
    scores = jnp.where(mask[None, None], scores, -1e+30)
    weights = jnp.exp(scores)
    weights = weights / lax.optimization_barrier(jnp.sum(weights, axis=-1, keepdims=True))
    attended = jnp.einsum('kgij,jkp->ikgp', weights, values, precision=highest)
    return (ssm_out.reshape(row_count, head_count * width), attended.reshape(row_count, query_count * width))

def core_apply(seg_ids, inputs, params):
    return mixer_core(*inputs, seg_ids, *params)

def reference(hidden_in, grad_out, segments, norm_gain, mamba_in, step_in, attn_in, conv_taps, conv_bias, step_bias, log_decay, skip_gain, gated_gain, mamba_out, attn_out, ffn_gain, gate_up, down_proj):
    x_width = DI // N_SEQ
    head_share = MH // N_SEQ
    query_share = QH * HD // N_SEQ
    owners = [group * KVH // N_SEQ for group in range(N_SEQ)]
    first_gain = norm_gain.astype(jnp.float32)
    mixer_gain = gated_gain.astype(jnp.float32)
    second_gain = ffn_gain.astype(jnp.float32)
    bf_type = jnp.bfloat16
    fl_type = jnp.float32

    def one_pack(totals, data):
        tok_in, cot_in, seg_ids = data
        residual = tok_in.astype(fl_type)
        first_scale = rms_scale(residual)
        first_norm = residual * first_scale
        normed = (first_norm * first_gain).astype(bf_type)
        projected = jnp.dot(normed, mamba_in, preferred_element_type=fl_type)
        gate_raw = projected[:, :DI]
        conv_in = projected[:, DI:].astype(bf_type)
        step_raw = jnp.dot(normed, step_in, preferred_element_type=fl_type).astype(bf_type)
        qkv_out = jnp.dot(normed, attn_in, preferred_element_type=fl_type).astype(bf_type)
        query_all = qkv_out[:, :QH * HD]
        key_part = qkv_out[:, QH * HD:(QH + KVH) * HD].reshape(LEN, KVH, HD)
        value_part = qkv_out[:, (QH + KVH) * HD:].reshape(LEN, KVH, HD)
        kv_pairs = jnp.concatenate([key_part, value_part], axis=2)
        ssm_parts, attn_parts, pullers = ([], [], [])
        for group in range(N_SEQ):
            x_cols = slice(group * x_width, (group + 1) * x_width)
            head_cols = slice(group * head_share, (group + 1) * head_share)
            taps = jnp.concatenate([conv_taps[:, x_cols], conv_taps[:, DI:]], axis=1)
            tap_bias = jnp.concatenate([conv_bias[x_cols], conv_bias[DI:]])
            inputs = (conv_in[:, x_cols].astype(fl_type), conv_in[:, DI:].astype(fl_type), step_raw[:, head_cols].astype(fl_type), query_all[:, group * query_share:(group + 1) * query_share].astype(fl_type), kv_pairs[:, owners[group]].astype(fl_type))
            params = (taps, tap_bias, step_bias[head_cols], log_decay[head_cols], skip_gain[head_cols])
            (ssm_group, attn_group), pull_back = jax.vjp(partial(core_apply, seg_ids), inputs, params)
            ssm_parts.append(ssm_group.astype(bf_type))
            attn_parts.append(attn_group.astype(bf_type))
            pullers.append(pull_back)
        scan_out = jnp.concatenate(ssm_parts, axis=1)
        attn_mix = jnp.concatenate(attn_parts, axis=1)
        scan_float = scan_out.astype(fl_type)
        gate_act = jax.nn.silu(gate_raw)
        gated = scan_float * gate_act
        gated_scale = rms_scale(gated)
        gated_norm = gated * gated_scale
        gated_b = (gated_norm * mixer_gain).astype(bf_type)
        mixed = residual + jnp.dot(gated_b, mamba_out, preferred_element_type=fl_type) + jnp.dot(attn_mix, attn_out, preferred_element_type=fl_type)
        second_scale = rms_scale(mixed)
        second_norm = mixed * second_scale
        ffn_in = (second_norm * second_gain).astype(bf_type)
        gate_vals = jnp.dot(ffn_in, gate_up, preferred_element_type=fl_type)
        gate_lin = gate_vals[:, :FF]
        up_lin = gate_vals[:, FF:]
        ffn_act = (jax.nn.silu(gate_lin) * up_lin).astype(bf_type)
        layer_out = (mixed + jnp.dot(ffn_act, down_proj, preferred_element_type=fl_type)).astype(bf_type)
        cot_float = cot_in.astype(fl_type)
        g_down = jnp.dot(ffn_act.T, cot_in, preferred_element_type=fl_type)
        d_act = jnp.dot(cot_in, down_proj.T, preferred_element_type=fl_type)
        d_ffn = jnp.concatenate([d_act * up_lin * swish_slope(gate_lin), d_act * jax.nn.silu(gate_lin)], axis=1).astype(bf_type)
        g_gate_up = jnp.dot(ffn_in.T, d_ffn, preferred_element_type=fl_type)
        d_ffn_in = jnp.dot(d_ffn, gate_up.T, preferred_element_type=fl_type)
        g_ffn_gain = lax.optimization_barrier(jnp.sum(d_ffn_in * second_norm, axis=0))
        d_second = d_ffn_in * second_gain
        d_mixed = cot_float + second_scale * (d_second - second_norm * lax.optimization_barrier(jnp.mean(d_second * second_norm, axis=-1, keepdims=True)))
        d_mixed_b = d_mixed.astype(bf_type)
        g_attn_out = jnp.dot(attn_mix.T, d_mixed_b, preferred_element_type=fl_type)
        d_attn_mix = jnp.dot(d_mixed_b, attn_out.T, preferred_element_type=fl_type).astype(bf_type)
        g_mamba_out = jnp.dot(gated_b.T, d_mixed_b, preferred_element_type=fl_type)
        d_gated_b = jnp.dot(d_mixed_b, mamba_out.T, preferred_element_type=fl_type)
        g_gated_gain = lax.optimization_barrier(jnp.sum(d_gated_b * gated_norm, axis=0))
        d_gnorm = d_gated_b * mixer_gain
        d_gated = gated_scale * (d_gnorm - gated_norm * lax.optimization_barrier(jnp.mean(d_gnorm * gated_norm, axis=-1, keepdims=True)))
        d_scan = (d_gated * gate_act).astype(bf_type)
        d_gate_raw = d_gated * scan_float * swish_slope(gate_raw)
        x_grads, step_grads, query_grads = ([], [], [])
        bc_total = jnp.zeros((LEN, 2 * NST), fl_type)
        kv_totals = [jnp.zeros((LEN, 2 * HD), fl_type) for kv_head in range(KVH)]
        taps_total = jnp.zeros((KC, CONV_CH), fl_type)
        bias_total = jnp.zeros((CONV_CH,), fl_type)
        step_total = jnp.zeros((MH,), fl_type)
        decay_total = jnp.zeros((MH,), fl_type)
        skip_total = jnp.zeros((MH,), fl_type)
        for group in range(N_SEQ):
            x_cols = slice(group * x_width, (group + 1) * x_width)
            head_cols = slice(group * head_share, (group + 1) * head_share)
            cot_pair = (d_scan[:, x_cols].astype(fl_type), d_attn_mix[:, group * query_share:(group + 1) * query_share].astype(fl_type))
            grad_inputs, grad_params = pullers[group](cot_pair)
            x_grads.append(grad_inputs[0].astype(bf_type))
            bc_total = bc_total + lax.optimization_barrier(grad_inputs[1].astype(bf_type)).astype(fl_type)
            step_grads.append(grad_inputs[2].astype(bf_type))
            query_grads.append(grad_inputs[3].astype(bf_type))
            kv_totals[owners[group]] = kv_totals[owners[group]] + lax.optimization_barrier(grad_inputs[4].astype(bf_type)).astype(fl_type)
            taps_total = taps_total.at[:, x_cols].add(grad_params[0][:, :x_width])
            taps_total = taps_total.at[:, DI:].add(grad_params[0][:, x_width:])
            bias_total = bias_total.at[x_cols].add(grad_params[1][:x_width])
            bias_total = bias_total.at[DI:].add(grad_params[1][x_width:])
            step_total = step_total.at[head_cols].add(grad_params[2])
            decay_total = decay_total.at[head_cols].add(grad_params[3])
            skip_total = skip_total.at[head_cols].add(grad_params[4])
        d_proj = jnp.concatenate([d_gate_raw.astype(bf_type)] + x_grads + [bc_total.astype(bf_type)], axis=1)
        d_step = jnp.concatenate(step_grads, axis=1)
        key_grads = [kv_totals[kv_head][:, :HD] for kv_head in range(KVH)]
        value_grads = [kv_totals[kv_head][:, HD:] for kv_head in range(KVH)]
        d_qkv = jnp.concatenate(query_grads + [jnp.concatenate(key_grads, axis=1).astype(bf_type), jnp.concatenate(value_grads, axis=1).astype(bf_type)], axis=1)
        g_mamba_in = jnp.dot(normed.T, d_proj, preferred_element_type=fl_type)
        g_step_in = jnp.dot(normed.T, d_step, preferred_element_type=fl_type)
        g_attn_in = jnp.dot(normed.T, d_qkv, preferred_element_type=fl_type)
        d_normed = jnp.dot(d_proj, mamba_in.T, preferred_element_type=fl_type) + jnp.dot(d_step, step_in.T, preferred_element_type=fl_type) + jnp.dot(d_qkv, attn_in.T, preferred_element_type=fl_type)
        g_norm_gain = lax.optimization_barrier(jnp.sum(d_normed * first_norm, axis=0))
        d_first = d_normed * first_gain
        grad_tok = d_mixed + first_scale * (d_first - first_norm * lax.optimization_barrier(jnp.mean(d_first * first_norm, axis=-1, keepdims=True)))
        terms = (g_norm_gain, g_mamba_in, g_step_in, g_attn_in, taps_total, bias_total, step_total, decay_total, skip_total, g_gated_gain, g_mamba_out, g_attn_out, g_ffn_gain, g_gate_up, g_down)
        totals = jax.tree.map(lambda acc_val, term: acc_val + term, totals, terms)
        return (totals, (layer_out, grad_tok))
    zeros = (jnp.zeros((D,), fl_type), jnp.zeros((D, 2 * DI + 2 * NST), fl_type), jnp.zeros((D, MH), fl_type), jnp.zeros((D, (QH + 2 * KVH) * HD), fl_type), jnp.zeros((KC, CONV_CH), fl_type), jnp.zeros((CONV_CH,), fl_type), jnp.zeros((MH,), fl_type), jnp.zeros((MH,), fl_type), jnp.zeros((MH,), fl_type), jnp.zeros((DI,), fl_type), jnp.zeros((DI, D), fl_type), jnp.zeros((QH * HD, D), fl_type), jnp.zeros((D,), fl_type), jnp.zeros((D, 2 * FF), fl_type), jnp.zeros((FF, D), fl_type))
    totals, stacked = lax.scan(one_pack, zeros, (hidden_in, grad_out, segments))
    return (stacked[0], stacked[1], totals[0], totals[1], totals[2], totals[3], totals[4], totals[5], totals[6], totals[7], totals[8], totals[9], totals[10], totals[11], totals[12], totals[13], totals[14])
```

```python
from functools import partial
import math

import jax
import jax.numpy as jnp
from jax import lax
from jax.sharding import PartitionSpec as P

MH = 24
HD = 64
NST = 128
KC = 4
QH = 8
KVH = 2
FF = 2048
DI = 1536


EPS = 1e-05
ROPE_THETA = 10000.0


def rms_scale(values):
    return lax.rsqrt(jnp.mean(values * values, axis=-1, keepdims=True) + EPS)


def swish_slope(values):
    sigma = jax.nn.sigmoid(values)
    return sigma * (1.0 + values * (1.0 - sigma))


def seq_gather(array):
    return lax.all_gather(array, "seq", axis=0, tiled=True)


def seq_exchange(blocks):
    return lax.all_to_all(blocks, "seq", split_axis=0, concat_axis=0, tiled=True)


def seq_reduce(partial_sums):
    seq_count = lax.axis_size("seq")
    blocks = partial_sums.reshape(seq_count, -1, partial_sums.shape[1])
    return jnp.sum(seq_exchange(blocks).astype(jnp.float32), axis=0)


def two_terms(column):
    high = column.astype(jnp.bfloat16)
    low = (column - high.astype(jnp.float32)).astype(jnp.bfloat16)
    return jnp.concatenate(
        [high, low, jnp.zeros((column.shape[0], 126), jnp.bfloat16)], axis=1
    )


def from_terms(terms):
    return terms[:, :1] + terms[:, 1:2]


def core_inputs(seg_ids, inputs, params):
    pre_conv, step_raw, query_in, key_in = inputs
    taps, tap_bias, step_bias, log_decay = params
    row_count = pre_conv.shape[0]
    tap_count = taps.shape[0]
    accum = tap_bias[None, :] + taps[tap_count - 1][None, :] * pre_conv
    for lag_step in range(1, tap_count):
        moved = jnp.concatenate(
            [
                jnp.zeros((lag_step, pre_conv.shape[1]), pre_conv.dtype),
                pre_conv[: row_count - lag_step],
            ],
            axis=0,
        )
        prior = jnp.concatenate(
            [jnp.full((lag_step,), -1, jnp.int32), seg_ids[: row_count - lag_step]]
        )
        same_seq = (prior == seg_ids)[:, None]
        accum = accum + taps[tap_count - 1 - lag_step][None, :] * jnp.where(same_seq, moved, 0.0)
    activated = jax.nn.silu(accum)
    step = jax.nn.softplus(step_raw + step_bias[None, :])
    log_step = -jnp.exp(log_decay)[None, :] * step
    positions = jnp.arange(row_count, dtype=jnp.int32)
    first_count = jnp.sum((seg_ids == 0).astype(jnp.int32))
    place = (positions - jnp.where(seg_ids == 0, 0, first_count)).astype(jnp.float32)
    half = HD // 2
    freqs = jnp.exp(-math.log(ROPE_THETA) * 2.0 * jnp.arange(half, dtype=jnp.float32) / HD)
    angles = place[:, None] * freqs[None, :]
    cosine = jnp.cos(angles)[:, None, :]
    sine = jnp.sin(angles)[:, None, :]

    def rotate(tensor):
        heads = tensor.reshape(row_count, -1, HD)
        first_half = heads[..., :half]
        second_half = heads[..., half:]
        return jnp.concatenate(
            [first_half * cosine - second_half * sine, second_half * cosine + first_half * sine],
            axis=-1,
        ).reshape(tensor.shape)

    return activated, step, log_step, rotate(query_in), rotate(key_in)


def shards(
    hidden_in,
    grad_out,
    segments,
    norm_gain,
    mamba_in,
    step_in,
    attn_in,
    conv_taps,
    conv_bias,
    step_bias,
    log_decay,
    skip_gain,
    gated_gain,
    mamba_out,
    attn_out,
    ffn_gain,
    gate_up,
    down_proj,
):
    bf_type = jnp.bfloat16
    fl_type = jnp.float32
    seq_count = lax.axis_size("seq")
    seq_index = lax.axis_index("seq")
    fsdp_count = lax.axis_size("fsdp")
    block_rows = hidden_in.shape[1]
    model = hidden_in.shape[2]
    rows = block_rows * seq_count
    own_rows = model // fsdp_count
    x_width = DI // seq_count
    head_share = MH // seq_count
    query_width = QH * HD // seq_count
    query_share = QH // seq_count
    ff_width = FF // seq_count
    col_width = model // seq_count
    owners = [group * KVH // seq_count for group in range(seq_count)]
    owner = seq_index * KVH // seq_count
    gain_own = DI // fsdp_count
    gain_cols = -(-gain_own // own_rows)

    def cols(array, start, size):
        return lax.dynamic_slice_in_dim(array, start, size, 1)

    gain_pad = jnp.pad(gated_gain, (0, gain_cols * own_rows - gain_own))
    in_parts = [
        cols(mamba_in, seq_index * x_width, x_width),
        cols(mamba_in, DI + seq_index * x_width, x_width),
        mamba_in[:, 2 * DI :],
        cols(attn_in, seq_index * query_width, query_width),
        cols(attn_in, QH * HD + owner * HD, HD),
        cols(attn_in, (QH + KVH) * HD + owner * HD, HD),
        cols(step_in, seq_index * head_share, head_share),
        norm_gain[:, None],
        ffn_gain[:, None],
        gain_pad.reshape(gain_cols, own_rows).T,
    ]
    main_width = 2 * x_width + 2 * NST + query_width + 2 * HD
    pad_width = 128 - head_share - 2 - gain_cols
    in_pack = jnp.concatenate(in_parts + [jnp.zeros((own_rows, pad_width), bf_type)], axis=1)
    out_cols = jnp.concatenate(
        [
            cols(mamba_out, seq_index * col_width, col_width),
            cols(attn_out, seq_index * col_width, col_width),
            cols(down_proj, seq_index * col_width, col_width),
        ],
        axis=0,
    )
    chunks = out_cols.shape[0] // own_rows
    big_pack = jnp.concatenate(
        [
            cols(gate_up, seq_index * ff_width, ff_width),
            cols(gate_up, FF + seq_index * ff_width, ff_width),
        ]
        + [out_cols[at * own_rows : (at + 1) * own_rows] for at in range(chunks)],
        axis=1,
    )
    hidden_all = seq_gather(hidden_in[0])
    in_all = lax.all_gather(in_pack, "fsdp", axis=0, tiled=True)
    big_all = lax.all_gather(big_pack, "fsdp", axis=0, tiled=True)
    cot_all = seq_gather(grad_out[0])
    gain_at = main_width + head_share
    first_gain = in_all[:, gain_at].astype(fl_type)
    second_gain = in_all[:, gain_at + 1].astype(fl_type)
    gated_gains = (
        in_all[:, gain_at + 2 : gain_at + 2 + gain_cols]
        .reshape(fsdp_count, own_rows, gain_cols)
        .transpose(0, 2, 1)
        .reshape(fsdp_count, gain_cols * own_rows)[:, :gain_own]
        .reshape(DI)
    )
    mixer_gain = lax.dynamic_slice_in_dim(gated_gains, seq_index * x_width, x_width, 0).astype(
        fl_type
    )
    w_gate_up = big_all[:, : 2 * ff_width]
    out_all = (
        big_all[:, 2 * ff_width :]
        .reshape(fsdp_count, own_rows, chunks, col_width)
        .transpose(0, 2, 1, 3)
        .reshape(fsdp_count, chunks * own_rows, col_width)
    )
    attn_own = QH * HD // fsdp_count
    out_send = jnp.concatenate(
        [
            out_all[:, :gain_own].reshape(seq_count, x_width, col_width),
            out_all[:, gain_own : gain_own + attn_own].reshape(seq_count, query_width, col_width),
            out_all[:, gain_own + attn_own :].reshape(seq_count, ff_width, col_width),
        ],
        axis=1,
    )
    out_w = seq_exchange(out_send).transpose(1, 0, 2).reshape(x_width + query_width + ff_width, model)
    w_mamba_out = out_w[:x_width]
    w_attn_out = out_w[x_width : x_width + query_width]
    w_down = out_w[x_width + query_width :]

    res_all = hidden_all.astype(fl_type)
    normed = (res_all * rms_scale(res_all) * first_gain).astype(bf_type)
    projected = jnp.dot(normed, in_all, preferred_element_type=fl_type)
    gate_raw = projected[:, :x_width]
    inputs_b = projected[:, x_width:].astype(bf_type).astype(fl_type)
    conv_width = x_width + 2 * NST
    conv_in = inputs_b[:, :conv_width]
    query_in = inputs_b[:, conv_width : conv_width + query_width]
    key_in = inputs_b[:, conv_width + query_width : conv_width + query_width + HD]
    value_b = inputs_b[:, conv_width + query_width + HD : conv_width + query_width + 2 * HD].astype(
        bf_type
    )
    step_at = conv_width + query_width + 2 * HD
    step_raw = inputs_b[:, step_at : step_at + head_share]
    seg_ids = segments[0]
    taps = jnp.concatenate(
        [cols(conv_taps, seq_index * x_width, x_width), conv_taps[:, DI:]], axis=1
    )
    tap_bias = jnp.concatenate(
        [lax.dynamic_slice_in_dim(conv_bias, seq_index * x_width, x_width, 0), conv_bias[DI:]]
    )
    params = (
        taps,
        tap_bias,
        lax.dynamic_slice_in_dim(step_bias, seq_index * head_share, head_share, 0),
        lax.dynamic_slice_in_dim(log_decay, seq_index * head_share, head_share, 0),
    )
    skip = lax.dynamic_slice_in_dim(skip_gain, seq_index * head_share, head_share, 0)
    (activated, step, log_step, queries, keys), pull_back = jax.vjp(
        partial(core_inputs, seg_ids), (conv_in, step_raw, query_in, key_in), params
    )
    positions = jnp.arange(rows, dtype=jnp.int32)
    causal = positions[:, None] >= positions[None, :]
    mask = causal & (seg_ids[:, None] == seg_ids[None, :])
    highest = lax.Precision.HIGHEST
    x_all = activated[:, :x_width]
    b_mat = activated[:, x_width : x_width + NST].astype(bf_type)
    c_mat = activated[:, x_width + NST :].astype(bf_type)
    x_heads = x_all.reshape(rows, head_share, HD).transpose(1, 0, 2)
    step_t = step.T
    cum_t = jnp.dot(log_step.T, causal.T.astype(fl_type), precision=highest)
    inner = jnp.einsum("tn,pn->tp", c_mat, b_mat, preferred_element_type=fl_type)
    decay = jnp.exp(jnp.where(mask[None], cum_t[:, :, None] - cum_t[:, None, :], -1e30))
    kernel_b = (inner[None] * decay).astype(bf_type)
    x_step = (x_heads * step_t[:, :, None]).astype(bf_type)
    scan_y = jnp.einsum("htp,hpd->htd", kernel_b, x_step, preferred_element_type=fl_type)
    ssm = scan_y + skip[:, None, None] * x_heads
    scan_float = (
        ssm.astype(bf_type).transpose(1, 0, 2).reshape(rows, x_width).astype(fl_type)
    )
    key_b = keys.astype(bf_type)
    q_heads = queries.reshape(rows, query_share, HD).transpose(1, 0, 2)
    scores = jnp.einsum("hid,jd->hij", q_heads, keys, precision=highest) * (1.0 / math.sqrt(HD))
    weights = jnp.exp(jnp.where(mask[None], scores, -1e30))
    weights = weights / jnp.sum(weights, axis=-1, keepdims=True)
    weights_b = weights.astype(bf_type)
    attended = jnp.einsum("hij,jd->hid", weights_b, value_b, preferred_element_type=fl_type)
    attn_mix = attended.astype(bf_type).transpose(1, 0, 2).reshape(rows, query_width)

    gate_act = jax.nn.silu(gate_raw)
    gated = scan_float * gate_act
    square_part = jnp.sum(gated * gated, axis=-1, keepdims=True)
    gated_un = (gated * mixer_gain).astype(bf_type)
    mix_parts = jnp.concatenate(
        [
            jnp.dot(gated_un, w_mamba_out, preferred_element_type=fl_type).astype(bf_type),
            jnp.dot(attn_mix, w_attn_out, preferred_element_type=fl_type).astype(bf_type),
            two_terms(square_part),
        ],
        axis=1,
    )
    mix_sum = seq_reduce(mix_parts)
    residual = hidden_in[0].astype(fl_type)
    gated_scale = lax.rsqrt(from_terms(mix_sum[:, 2 * model :]) / DI + EPS)
    mamba_part = gated_scale * mix_sum[:, :model]
    mixed = residual + mamba_part + mix_sum[:, model : 2 * model]
    second_scale = rms_scale(mixed)
    second_norm = mixed * second_scale
    ffn_own = (second_norm * second_gain).astype(bf_type)
    ffn_got = seq_gather(jnp.concatenate([ffn_own, two_terms(gated_scale)], axis=1))
    ffn_in = ffn_got[:, :model]
    scale_all = from_terms(ffn_got[:, model:].astype(fl_type))
    gate_vals = jnp.dot(ffn_in, w_gate_up, preferred_element_type=fl_type)
    gate_lin = gate_vals[:, :ff_width]
    up_lin = gate_vals[:, ff_width:]
    ffn_act = (jax.nn.silu(gate_lin) * up_lin).astype(bf_type)
    d_act = jnp.einsum("td,fd->tf", cot_all, w_down, preferred_element_type=fl_type)
    d_ffn = jnp.concatenate(
        [d_act * up_lin * swish_slope(gate_lin), d_act * jax.nn.silu(gate_lin)], axis=1
    ).astype(bf_type)
    ffn_sum = seq_reduce(
        jnp.concatenate(
            [
                jnp.dot(ffn_act, w_down, preferred_element_type=fl_type).astype(bf_type),
                jnp.einsum("tf,df->td", d_ffn, w_gate_up, preferred_element_type=fl_type).astype(
                    bf_type
                ),
            ],
            axis=1,
        )
    )
    layer_out = (mixed + ffn_sum[:, :model]).astype(bf_type)
    d_ffn_in = ffn_sum[:, model:]
    g_down = jnp.einsum("tf,td->fd", ffn_act, cot_all, preferred_element_type=fl_type)
    g_gate_up = jnp.einsum("td,tf->df", ffn_in, d_ffn, preferred_element_type=fl_type)
    g_ffn_gain = jnp.sum(d_ffn_in * second_norm, axis=0)
    d_second = d_ffn_in * second_gain
    d_mixed = grad_out[0].astype(fl_type) + second_scale * (
        d_second - second_norm * jnp.mean(d_second * second_norm, axis=-1, keepdims=True)
    )
    d_mixed_own = d_mixed.astype(bf_type)
    mean_own = jnp.sum(d_mixed_own.astype(fl_type) * mamba_part, axis=-1, keepdims=True) / DI
    mixed_got = seq_gather(jnp.concatenate([d_mixed_own, two_terms(mean_own)], axis=1))
    d_mixed_b = mixed_got[:, :model]
    mean_all = from_terms(mixed_got[:, model:].astype(fl_type))
    gated_norm = gated * scale_all
    gated_b = (gated_norm * mixer_gain).astype(bf_type)
    g_attn_out = jnp.einsum("tq,td->qd", attn_mix, d_mixed_b, preferred_element_type=fl_type)
    g_mamba_out = jnp.einsum("ti,td->id", gated_b, d_mixed_b, preferred_element_type=fl_type)
    d_attn = jnp.einsum("td,qd->tq", d_mixed_b, w_attn_out, preferred_element_type=fl_type)
    d_gated_b = jnp.einsum("td,id->ti", d_mixed_b, w_mamba_out, preferred_element_type=fl_type)
    g_gated_gain = jnp.sum(d_gated_b * gated_norm, axis=0)
    d_gated = scale_all * (d_gated_b * mixer_gain - gated_norm * mean_all)
    d_scan = (d_gated * gate_act).astype(bf_type)
    d_gate_raw = d_gated * scan_float * swish_slope(gate_raw)

    g_rows = jnp.concatenate([g_mamba_out, g_attn_out, g_down], axis=0).astype(bf_type)
    g_got = seq_exchange(
        g_rows.reshape(g_rows.shape[0], seq_count, col_width).transpose(1, 0, 2)
    )
    g_out = jnp.concatenate(
        [
            g_got[:, :x_width].reshape(fsdp_count, gain_own, col_width),
            g_got[:, x_width : x_width + query_width].reshape(fsdp_count, attn_own, col_width),
            g_got[:, x_width + query_width :].reshape(fsdp_count, FF // fsdp_count, col_width),
        ],
        axis=1,
    )
    g_out = (
        g_out.reshape(fsdp_count, chunks, own_rows, col_width)
        .transpose(0, 2, 1, 3)
        .reshape(model, chunks * col_width)
    )
    big_shard = lax.psum_scatter(
        jnp.concatenate([g_gate_up.astype(bf_type), g_out], axis=1),
        "fsdp",
        scatter_dimension=0,
        tiled=True,
    )
    big_grads = lax.all_gather(big_shard, "seq", axis=0, tiled=False).astype(fl_type)

    d_att = d_attn.astype(bf_type).reshape(rows, query_share, HD).transpose(1, 0, 2)
    d_weights = jnp.einsum("hid,jd->hij", d_att, value_b, preferred_element_type=fl_type)
    inner_sum = jnp.sum(d_att.astype(fl_type) * attended, axis=-1, keepdims=True)
    d_scores = (weights * (d_weights - inner_sum) * (1.0 / math.sqrt(HD))).astype(bf_type)
    d_queries = jnp.einsum("hij,jd->hid", d_scores, key_b, preferred_element_type=fl_type)
    d_keys = jnp.einsum(
        "hij,hid->jd", d_scores, q_heads.astype(bf_type), preferred_element_type=fl_type
    )
    d_value = jnp.einsum("hij,hid->jd", weights_b, d_att, preferred_element_type=fl_type)
    d_y = d_scan.reshape(rows, head_share, HD).transpose(1, 0, 2)
    d_y_float = d_y.astype(fl_type)
    d_kernel = jnp.einsum("htd,hpd->htp", d_y, x_step, preferred_element_type=fl_type)
    d_inner = jnp.sum(d_kernel * decay, axis=0).astype(bf_type)
    d_x_step = jnp.einsum("htp,htd->hpd", kernel_b, d_y, preferred_element_type=fl_type)
    d_c = jnp.dot(d_inner, b_mat, preferred_element_type=fl_type)
    d_b = jnp.einsum("tp,tn->pn", d_inner, c_mat, preferred_element_type=fl_type)
    d_x = step_t[:, :, None] * d_x_step + skip[:, None, None] * d_y_float
    g_skip = jnp.sum(d_y_float * x_heads, axis=(1, 2))
    d_step_direct = jnp.sum(x_heads * d_x_step, axis=-1)
    d_cum = jnp.sum(d_y_float * scan_y, axis=-1) - jnp.sum(
        x_step.astype(fl_type) * d_x_step, axis=-1
    )
    d_log_step = jnp.dot(d_cum, causal.astype(fl_type), precision=highest)
    (d_conv, d_step, d_query, d_key), grad_params = pull_back(
        (
            jnp.concatenate([d_x.transpose(1, 0, 2).reshape(rows, x_width), d_b, d_c], axis=1),
            d_step_direct.T,
            d_log_step.T,
            d_queries.transpose(1, 0, 2).reshape(rows, query_width),
            d_keys,
        )
    )
    d_in = jnp.concatenate(
        [
            d_gate_raw,
            d_conv,
            d_query,
            d_key,
            d_value,
            d_step,
            jnp.zeros((rows, 128 - head_share), fl_type),
        ],
        axis=1,
    ).astype(bf_type)
    g_in = jnp.einsum("td,tc->dc", normed, d_in, preferred_element_type=fl_type)
    in_shard = lax.psum_scatter(g_in.astype(bf_type), "fsdp", scatter_dimension=0, tiled=True)
    in_grads = lax.all_gather(in_shard, "seq", axis=0, tiled=False).astype(fl_type)
    d_normed = seq_reduce(
        jnp.einsum("tc,dc->td", d_in, in_all, preferred_element_type=fl_type).astype(bf_type)
    )
    first_scale = rms_scale(residual)
    first_norm = residual * first_scale
    g_norm_gain = jnp.sum(d_normed * first_norm, axis=0)
    d_first = d_normed * first_gain
    grad_tok = d_mixed + first_scale * (
        d_first - first_norm * jnp.mean(d_first * first_norm, axis=-1, keepdims=True)
    )

    def placed_cols(block, width, start):
        return lax.dynamic_update_slice_in_dim(
            jnp.zeros(block.shape[:-1] + (width,), fl_type), block, start, block.ndim - 1
        )

    conv_channels = DI + 2 * NST
    taps_bias = jnp.concatenate([grad_params[0], grad_params[1][None]], axis=0)
    taps_total = jnp.concatenate(
        [
            placed_cols(taps_bias[:, :x_width], DI, seq_index * x_width),
            taps_bias[:, x_width:],
        ],
        axis=1,
    )
    heads_total = placed_cols(
        jnp.stack([grad_params[2], grad_params[3], g_skip]), MH, seq_index * head_share
    )
    gated_total = placed_cols(g_gated_gain, DI, seq_index * x_width)
    small = lax.psum(
        jnp.concatenate(
            [
                taps_total.reshape(-1),
                gated_total,
                g_norm_gain,
                g_ffn_gain,
                heads_total.reshape(-1),
            ]
        ),
        ("seq", "fsdp"),
    )
    at = (KC + 1) * conv_channels
    taps_sum = small[:at].reshape(KC + 1, conv_channels)
    fsdp_index = lax.axis_index("fsdp")
    gated_sum = lax.dynamic_slice_in_dim(small, at + fsdp_index * gain_own, gain_own, 0)
    at = at + DI
    norm_sum = lax.dynamic_slice_in_dim(small, at + fsdp_index * own_rows, own_rows, 0)
    at = at + model
    ffn_gain_sum = lax.dynamic_slice_in_dim(small, at + fsdp_index * own_rows, own_rows, 0)
    at = at + model
    heads_sum = small[at : at + 3 * MH].reshape(3, MH)

    def side(array):
        return jnp.concatenate([array[group] for group in range(seq_count)], axis=1)

    def owned(start):
        slots = []
        for kv_head in range(KVH):
            users = [group for group in range(seq_count) if owners[group] == kv_head]
            total = in_grads[users[0]][:, start : start + HD]
            for group in users[1:]:
                total = total + in_grads[group][:, start : start + HD]
            slots.append(total)
        return slots

    q_at = 2 * x_width + 2 * NST
    grad_mamba_in = jnp.concatenate(
        [
            side(in_grads[:, :, :x_width]),
            side(in_grads[:, :, x_width : 2 * x_width]),
            jnp.sum(in_grads[:, :, 2 * x_width : q_at], axis=0),
        ],
        axis=1,
    )
    k_at = q_at + query_width
    grad_attn_in = jnp.concatenate(
        [side(in_grads[:, :, q_at:k_at])] + owned(k_at) + owned(k_at + HD), axis=1
    )
    grad_step_in = side(in_grads[:, :, main_width : main_width + head_share])
    grad_gate_up = jnp.concatenate(
        [side(big_grads[:, :, :ff_width]), side(big_grads[:, :, ff_width : 2 * ff_width])], axis=1
    )
    out_grads = jnp.concatenate(
        [
            side(
                big_grads[
                    :,
                    :,
                    2 * ff_width + at * col_width : 2 * ff_width + (at + 1) * col_width,
                ]
            )
            for at in range(chunks)
        ],
        axis=0,
    )
    return (
        layer_out[None],
        grad_tok[None],
        norm_sum,
        grad_mamba_in,
        grad_step_in,
        grad_attn_in,
        taps_sum[:KC],
        taps_sum[KC],
        heads_sum[0],
        heads_sum[1],
        heads_sum[2],
        gated_sum,
        out_grads[:gain_own],
        out_grads[gain_own : gain_own + attn_own],
        ffn_gain_sum,
        grad_gate_up,
        out_grads[gain_own + attn_own :],
    )


def solution(mesh):
    placed = (
        P("fsdp", "seq", None),
        P("fsdp", "seq", None),
        P("fsdp", None),
        P("fsdp"),
        P("fsdp", None),
        P("fsdp", None),
        P("fsdp", None),
        P(),
        P(),
        P(),
        P(),
        P(),
        P("fsdp"),
        P("fsdp", None),
        P("fsdp", None),
        P("fsdp"),
        P("fsdp", None),
        P("fsdp", None),
    )
    return jax.shard_map(
        shards,
        mesh=mesh,
        in_specs=placed,
        out_specs=(
            P("fsdp", "seq", None),
            P("fsdp", "seq", None),
            P("fsdp"),
            P("fsdp", None),
            P("fsdp", None),
            P("fsdp", None),
            P(),
            P(),
            P(),
            P(),
            P(),
            P("fsdp"),
            P("fsdp", None),
            P("fsdp", None),
            P("fsdp"),
            P("fsdp", None),
            P("fsdp", None),
        ),
        check_vma=False,
    )
```
